256 devices in a mesh: win: 8 (over z), sec: 32 (over x, y, core).
Axes of the slice: x: 4, y: 4, z: 8, core: 2. Of those that a mesh axis runs over, the one named last changes fastest.
Arguments:
- initial: bfloat16 [5, 16, 24, 512], P(None, 'win'), may hold values from -6 to 6
- props: bfloat16 [32, 8, 2, 256, 256], P('sec'), may hold values from -0.25 to 0.25
- screen: float32 [32, 16, 256], P('sec', 'win'), may hold values from -3.140625 to 3.140625
- links: int32 [32, 16, 6], P('sec', 'win'), may hold values from 0 to 15, as said below
- kinds: int32 [32, 16, 6], P('sec', 'win'), may hold values from 0 to 7
- counts: int32 [32, 16], P('sec', 'win'), may hold values from 1 to 6
Outputs:
- fields: bfloat16 [32, 5, 16, 24, 512], P('sec', None, 'win')
The draws below stay inside these ranges and needn't reach their ends.
Inputs may be any that keep to these rules, and one draw needn't show every extreme that they name: links[s, w, l] lies within w - 1 to w + 1.
All inputs are finite; a program needn't handle non-finite values.
Results may differ from the reference program's by a relative error of at most 0.033.
Values may be sent and summed in bfloat16 or wider, within the bound.
No kernel may reach another device: no remote copies, remote signals or barrier semaphores. Data moves between devices by JAX's collectives and lax.ppermute only.
A program may use at most 64 MiB of HBM per device.

```python
import jax
import jax.numpy as jnp
from jax import lax

K = 256
S = 24
F = 5
L = 6
NPROP = 8
W = 16
NSEC = 32


def draw_links(key, part):
    offsets = jax.random.randint(key, (NSEC, W, L), -1, 2)
    base = jnp.arange(W, dtype=jnp.int32)[None, :, None]
    return jnp.clip(base + offsets, 0, W - 1).astype(jnp.int32)


def with_ends(entries, key, least, largest):
    longest = entries.shape.index(max(entries.shape))
    spots = []
    for shift in (0, 1):
        where = [jax.random.randint(jax.random.fold_in(key, axis), (), 0, length) for axis, length in enumerate(entries.shape)]
        where[longest] = (where[longest] + shift) % entries.shape[longest]
        spots.append(tuple(where))
    return entries.at[spots[0]].set(least).at[spots[1]].set(largest)


def block_levels(rng, shape, pieces, low, high):
    level = 1.0
    for axis_at, blocks in pieces:
        steps = jax.random.uniform(jax.random.fold_in(jax.random.fold_in(rng, 6), axis_at), (blocks,), jnp.float32, low / len(pieces), high / len(pieces))
        level = level * jnp.repeat(jnp.exp(steps), shape[axis_at] // blocks).reshape((-1,) + (1,) * (len(shape) - 1 - axis_at))
    return level


def gaussian(own_key, shape, scale, limit, cuts=(), kind=jnp.bfloat16):
    entries = scale * jax.random.normal(own_key, shape, jnp.float32)
    if cuts:
        entries = entries * block_levels(own_key, shape, cuts, -0.22, 0.18)
    return jnp.clip(entries, -limit, limit).astype(kind)


def setup_inputs(seed: int = 0) -> dict:
    splits = jax.random.split(jax.random.key(seed), 7)
    return {
        "initial": gaussian(splits[0], (F, W, S, 2 * K), 1.0, 6.0, ((1, 8),)),
        "props": gaussian(splits[1], (NSEC, NPROP, 2, K, K), (2 * K) ** -0.5, 0.25, ((0, 32),)),
        "screen": jnp.clip(jax.random.uniform(splits[2], (NSEC, W, K), jnp.float32, -3.140625, 3.140625), -3.140625, 3.140625),
        "links": draw_links(jax.random.fold_in(splits[6], 71), 0),
        "kinds": with_ends(jax.random.randint(splits[4], (NSEC, W, L), 0, NPROP), jax.random.fold_in(splits[4], 1), 0, NPROP - 1).astype(jnp.int32),
        "counts": with_ends(jax.random.randint(splits[5], (NSEC, W), 1, L + 1), jax.random.fold_in(splits[5], 1), 1, L).astype(jnp.int32),
    }


def build_blocks(section_table):
    real_part = section_table[:, 0].astype(jnp.float32)
    imag_part = section_table[:, 1].astype(jnp.float32)
    upper = jnp.concatenate([real_part, imag_part], axis=-1)
    lower = jnp.concatenate([-imag_part, real_part], axis=-1)
    return jnp.concatenate([upper, lower], axis=-2)

def section_step(field, inputs):
    section_table, screen_phase, link_rows, kind_rows, count_rows = inputs
    blocks = build_blocks(section_table)
    field_wide = field.astype(jnp.float32)
    gathered = field_wide[:, link_rows]
    scaled = lax.rsqrt(count_rows.astype(jnp.float32))
    weighting = (jnp.arange(L)[None, :] < count_rows[:, None]).astype(jnp.float32) * scaled[:, None]
    total = jnp.zeros(field.shape, jnp.float32)
    for entry in range(NPROP):
        picked = weighting * (kind_rows == entry).astype(jnp.float32)
        mixed = jnp.einsum('wl,fwlsc->fwsc', picked, gathered, precision=lax.Precision.HIGHEST)
        total = total + jnp.einsum('fwsc,cd->fwsd', mixed, blocks[entry], precision=lax.Precision.HIGHEST)
    real_out = total[..., :K]
    imag_out = total[..., K:]
    cosine = jnp.cos(screen_phase)[None, :, None, :]
    sine_part = jnp.sin(screen_phase)[None, :, None, :]
    result = jnp.concatenate([real_out * cosine - imag_out * sine_part, real_out * sine_part + imag_out * cosine], axis=-1).astype(jnp.bfloat16)
    return (result, result)

def reference(initial, props, screen, links, kinds, counts):
    final_field, fields = lax.scan(section_step, initial, (props, screen, links, kinds, counts))
    return fields
```

```python
import functools

import jax
import jax.numpy as jnp
from jax import lax
from jax.experimental import pallas as pl
from jax.experimental.pallas import tpu as pltpu
from jax.sharding import PartitionSpec as P

ROWS = 8
LANES = 128
VMEM = pl.BlockSpec(memory_space=pltpu.VMEM)
SMEM = pl.BlockSpec(memory_space=pltpu.SMEM)
ANY = pl.BlockSpec(memory_space=pl.ANY)
LIMIT = pltpu.CompilerParams(vmem_limit_bytes=16 << 20)


def pack_kernel(entries, initial_ref, screen_ref, links_ref, kinds_ref, counts_ref, out_ref):
    fronts, own_windows, sources, width = initial_ref.shape
    core = lax.axis_index("sec") % 2
    first = lax.axis_index("win") * own_windows
    members = out_ref.shape[0]
    list_length = links_ref.shape[-1]
    per_front = sources // ROWS
    lane = lax.broadcasted_iota(jnp.int32, (1, width), 1)
    trig_rows, hit_rows = [], []
    for w in range(own_windows):
        count = counts_ref[0, w]
        scale = lax.rsqrt(jnp.full((1, width // 2), count, jnp.int32).astype(jnp.float32))
        angle = screen_ref[0, w : w + 1, :]
        trig = jnp.concatenate([jnp.cos(angle) * scale, jnp.sin(angle) * scale], axis=1)
        high = trig.astype(jnp.bfloat16)
        trig_rows += [high, (trig - high.astype(jnp.float32)).astype(jnp.bfloat16)]
        hits = jnp.zeros((1, width), jnp.float32)
        for l in range(list_length):
            spot = kinds_ref[0, w, l] * 3 + links_ref[0, w, l] - (first + w) + 1
            hits = hits + jnp.where((lane == spot) & (l < count), 1.0, 0.0)
        hit_rows.append(hits.astype(jnp.bfloat16))
    spare = jnp.zeros((ROWS - 3 * own_windows, width), jnp.bfloat16)
    tables = jnp.concatenate(trig_rows + hit_rows + [spare], axis=0)
    for member in range(members):
        if member < fronts * per_front:
            f, j = divmod(member, per_front)
            out_ref[member, :ROWS] = initial_ref[f, core, j * ROWS : (j + 1) * ROWS]
        else:
            out_ref[member, :ROWS] = jnp.zeros((ROWS, width), jnp.bfloat16)
        out_ref[member, ROWS:] = tables


def unpack_kernel(entries, coeffs, received_ref, field_ref, mix_ref, cs_ref, ds_ref):
    columns = received_ref.shape[0] // 2
    for z in range(columns):
        for core in range(2):
            block = received_ref[2 * z + core]
            window = 2 * z + core
            field_ref[window * ROWS : (window + 1) * ROWS] = block[:ROWS]
            wide = block.astype(jnp.float32)
            for w in range(2):
                at = pl.ds((2 * z + w) * ROWS, ROWS)
                trig = wide[ROWS + 2 * w : ROWS + 2 * w + 1] + wide[ROWS + 2 * w + 1 : ROWS + 2 * w + 2]
                cs_ref[core, at, :] = jnp.broadcast_to(trig[:, :coeffs], (ROWS, coeffs))
                ds_ref[core, at, :] = jnp.broadcast_to(trig[:, coeffs:], (ROWS, coeffs))
                hits = wide[ROWS + 4 + w : ROWS + 5 + w]
                for spot in range(3 * entries):
                    mix_ref[core, spot, at, :] = jnp.broadcast_to(
                        hits[:, spot : spot + 1], (ROWS, LANES)
                    ).astype(jnp.bfloat16)


def order_kernel(own_ref, other_ref, out_ref, sems):
    core = lax.axis_index("sec") % 2
    a = pltpu.make_async_copy(own_ref, out_ref.at[core], sems.at[0])
    b = pltpu.make_async_copy(other_ref, out_ref.at[1 - core], sems.at[1])
    a.start()
    b.start()
    a.wait()
    b.wait()


def stage_kernel(turn, entries, coeffs, x_ref, w_ref, mix_ref, cs_ref, ds_ref, kept_ref, y_ref, out_ref):
    del kept_ref
    points = x_ref.shape[0]
    pairs, sections, group, width = out_ref.shape
    repeat = width // LANES

    @pl.when(lax.axis_index("sec") // 2 == turn)
    def _():
        y_ref[...] = x_ref[...]
        zero = jnp.zeros((ROWS, width), jnp.float32)

        def one(section, carry):
            field = y_ref[...].astype(jnp.float32)
            low = jnp.concatenate([zero, field[:-ROWS]], axis=0)
            high = jnp.concatenate([field[ROWS:], zero], axis=0)
            tops, bottoms = [], []
            for entry in range(entries):
                hits = [
                    jnp.concatenate([mix_ref[section, 3 * entry + j]] * repeat, axis=1).astype(jnp.float32)
                    for j in range(3)
                ]
                mixed = (hits[0] * low + hits[1] * field + hits[2] * high).astype(jnp.bfloat16)
                re, im = mixed[:, :coeffs], mixed[:, coeffs:]
                tops += [re, -im]
                bottoms += [im, re]
            weights = w_ref[section]
            re = jnp.dot(jnp.concatenate(tops, axis=1), weights, preferred_element_type=jnp.float32)
            im = jnp.dot(jnp.concatenate(bottoms, axis=1), weights, preferred_element_type=jnp.float32)
            cs, ds = cs_ref[section], ds_ref[section]
            field = jnp.concatenate([re * cs - im * ds, re * ds + im * cs], axis=1).astype(jnp.bfloat16)
            y_ref[...] = field
            for pair in range(pairs):
                out_ref[pair, section] = field[pair * group : (pair + 1) * group]
            return carry

        lax.fori_loop(0, sections, one, 0)


def local(initial, props, screen, links, kinds, counts):
    fronts, own_windows, sources, width = initial.shape
    coeffs = width // 2
    entries = props.shape[1]
    columns = lax.axis_size("win")
    sections = lax.axis_size("sec")
    chips = sections // 2
    windows = own_windows * columns
    members = 2 * columns
    points = windows * ROWS
    used = fronts * sources // ROWS
    bf16, f32 = jnp.bfloat16, jnp.float32
    groups = [
        [w * sections + 2 * c + k for w in range(columns) for k in range(2)] for c in range(chips)
    ]

    own = props.reshape(entries * 2 * coeffs, coeffs)
    other = lax.ppermute(own, "sec", [(s, s ^ 1) for s in range(sections)])
    weights = pl.pallas_call(
        order_kernel,
        out_shape=jax.ShapeDtypeStruct((2,) + own.shape, bf16),
        in_specs=[ANY, ANY],
        out_specs=VMEM,
        scratch_shapes=[pltpu.SemaphoreType.DMA((2,))],
        compiler_params=LIMIT,
        name="order",
    )(own, other)

    payload = pl.pallas_call(
        functools.partial(pack_kernel, entries),
        out_shape=jax.ShapeDtypeStruct((members, 2 * ROWS, width), bf16),
        in_specs=[VMEM, VMEM, SMEM, SMEM, SMEM],
        out_specs=VMEM,
        compiler_params=LIMIT,
        name="pack",
    )(initial, screen, links, kinds, counts)
    received = lax.all_to_all(payload, ("win", "sec"), 0, 0, axis_index_groups=groups, tiled=True)
    field, mixing, cs, ds = pl.pallas_call(
        functools.partial(unpack_kernel, entries, coeffs),
        out_shape=(
            jax.ShapeDtypeStruct((points, width), bf16),
            jax.ShapeDtypeStruct((2, 3 * entries, points, LANES), bf16),
            jax.ShapeDtypeStruct((2, points, coeffs), f32),
            jax.ShapeDtypeStruct((2, points, coeffs), f32),
        ),
        in_specs=[VMEM],
        out_specs=(VMEM,) * 4,
        compiler_params=LIMIT,
        name="unpack",
    )(received)

    kept = jnp.zeros((columns, 2, own_windows * ROWS, width), bf16)
    for turn in range(chips):
        field, kept = pl.pallas_call(
            functools.partial(stage_kernel, turn, entries, coeffs),
            out_shape=(jax.ShapeDtypeStruct(field.shape, bf16), jax.ShapeDtypeStruct(kept.shape, bf16)),
            in_specs=[VMEM] * 6,
            out_specs=(VMEM, VMEM),
            input_output_aliases={5: 1},
            cost_estimate=pl.CostEstimate(
                flops=16 * entries * points * coeffs * coeffs, bytes_accessed=weights.size * 2, transcendentals=0
            ),
            compiler_params=LIMIT,
            name="stage",
        )(field, weights, mixing, cs, ds, kept)
        if turn + 1 < chips:
            field = lax.ppermute(field, "sec", [(2 * turn + k, 2 * turn + 2 + k) for k in range(2)])

    fields = lax.all_to_all(
        kept.reshape(members, own_windows * ROWS, width), ("win", "sec"), 0, 0, axis_index_groups=groups, tiled=True
    )
    fields = fields[:used].reshape(fronts, sources // ROWS, own_windows, ROWS, width)
    return fields.transpose(0, 2, 1, 3, 4).reshape(initial.shape)[None]


def solution(mesh):
    placed = (
        P(None, "win", None, None),
        P("sec", None, None, None, None),
        P("sec", "win", None),
        P("sec", "win", None),
        P("sec", "win", None),
        P("sec", "win"),
    )
    return jax.shard_map(
        local,
        mesh=mesh,
        in_specs=placed,
        out_specs=P("sec", None, "win", None, None),
        check_vma=False,
    )
```

```python
import functools

import jax
import jax.numpy as jnp
from jax import lax
from jax.experimental import pallas as pl
from jax.experimental.pallas import tpu as pltpu
from jax.sharding import PartitionSpec as P

ROWS = 8
LANES = 128
CHUNKS = 2
UNITS = 2
VMEM = pl.BlockSpec(memory_space=pltpu.VMEM)
HBM = pl.BlockSpec(memory_space=pltpu.HBM)
LIMIT = pltpu.CompilerParams(vmem_limit_bytes=16 << 20)


def pack_kernel(
    entries,
    initial_hbm, screen_hbm, links_hbm, kinds_hbm, counts_hbm, own_hbm, out_ref, weights_ref,
    initial_ref, screen_ref, links_ref, kinds_ref, counts_ref, sems,
):
    copies = [
        pltpu.make_async_copy(source, target, sems.at[i])
        for i, (source, target) in enumerate(
            (
                (counts_hbm, counts_ref),
                (kinds_hbm, kinds_ref),
                (links_hbm, links_ref),
                (screen_hbm, screen_ref),
                (initial_hbm, initial_ref),
                (own_hbm, weights_ref.at[lax.axis_index("sec") % 2]),
            )
        )
    ]
    for copy in copies:
        copy.start()
    for copy in copies[:-1]:
        copy.wait()
    fronts, own_windows, sources, width = initial_ref.shape
    core = lax.axis_index("sec") % 2
    first = lax.axis_index("win") * own_windows
    members = out_ref.shape[0]
    list_length = links_ref.shape[-1]
    per_front = sources // ROWS
    lane = lax.broadcasted_iota(jnp.int32, (1, width), 1)
    trig_rows, hit_rows = [], []
    for w in range(own_windows):
        count = counts_ref[0, w]
        scale = lax.rsqrt(jnp.full((1, width // 2), count, jnp.int32).astype(jnp.float32))
        angle = screen_ref[0, w : w + 1, :]
        trig = jnp.concatenate([jnp.cos(angle) * scale, jnp.sin(angle) * scale], axis=1)
        high = trig.astype(jnp.bfloat16)
        trig_rows += [high, (trig - high.astype(jnp.float32)).astype(jnp.bfloat16)]
        hits = jnp.zeros((1, width), jnp.float32)
        for l in range(list_length):
            spot = kinds_ref[0, w, l] * 3 + links_ref[0, w, l] - (first + w) + 1
            hits = hits + jnp.where((lane == spot) & (l < count), 1.0, 0.0)
        hit_rows.append(hits.astype(jnp.bfloat16))
    spare = jnp.zeros((ROWS - 3 * own_windows, width), jnp.bfloat16)
    tables = jnp.concatenate(trig_rows + hit_rows + [spare], axis=0)
    for member in range(members):
        if member < fronts * per_front:
            f, j = divmod(member, per_front)
            out_ref[member, :ROWS] = initial_ref[f, core, j * ROWS : (j + 1) * ROWS]
        else:
            out_ref[member, :ROWS] = jnp.zeros((ROWS, width), jnp.bfloat16)
        out_ref[member, ROWS:] = tables
    copies[-1].wait()


def unpack_kernel(entries, coeffs, received_ref, other_ref, field_refs, mix_ref, cs_ref, ds_ref, weights_ref, sem):
    copy = pltpu.make_async_copy(other_ref, weights_ref.at[1 - lax.axis_index("sec") % 2], sem)
    copy.start()
    columns = received_ref.shape[0] // 2
    own_windows = 2
    part = ROWS // len(field_refs)
    for z in range(columns):
        blocks = [received_ref[2 * z + core].astype(jnp.float32) for core in range(2)]
        at = pl.ds(own_windows * part * z, own_windows * part)
        for chunk, field_ref in enumerate(field_refs):
            rows = [block[chunk * part : (chunk + 1) * part] for block in blocks]
            field_ref[at, :] = jnp.concatenate(rows, axis=0).astype(jnp.bfloat16)
        for core in range(2):
            trigs, hits = [], []
            for w in range(own_windows):
                row = ROWS + 2 * w
                trig = blocks[core][row : row + 1] + blocks[core][row + 1 : row + 2]
                trigs.append(jnp.broadcast_to(trig, (part, 2 * coeffs)))
                row = ROWS + 2 * own_windows + w
                hits.append(jnp.broadcast_to(blocks[core][row : row + 1, :LANES], (part, LANES)))
            trig = jnp.concatenate(trigs, axis=0)
            cs_ref[core, at, :] = trig[:, :coeffs]
            ds_ref[core, at, :] = trig[:, coeffs:]
            hit = jnp.concatenate(hits, axis=0)
            for spot in range(3 * entries):
                mix_ref[core, spot, at, :] = jnp.broadcast_to(hit[:, spot : spot + 1], (own_windows * part, LANES))
    copy.wait()


def repack_kernel(got_ref, out_ref):
    fronts, own_windows, sources, width = out_ref.shape
    per_front = sources // ROWS
    chunks = got_ref.shape[1] // (own_windows * ROWS // CHUNKS)
    part = ROWS // chunks
    for f in range(fronts):
        for j in range(per_front):
            block = got_ref[f * per_front + j].astype(jnp.float32)
            for w in range(own_windows):
                rows = [block[(c * own_windows + w) * part : (c * own_windows + w + 1) * part] for c in range(chunks)]
                out_ref[f, w, j * ROWS : (j + 1) * ROWS] = jnp.concatenate(rows, axis=0).astype(jnp.bfloat16)


def stage_kernel(turn, chunk, entries, coeffs, x_ref, w_ref, mix_ref, cs_ref, ds_ref, y_ref, out_ref, *sums):
    points, width = x_ref.shape
    pairs, sections, group, _ = out_ref.shape
    step = ROWS // CHUNKS
    group = group // CHUNKS
    repeat = width // LANES

    @pl.when(lax.axis_index("sec") // 2 == turn)
    def _():
        y_ref[...] = x_ref[...]

        def one(section, carry):
            field = y_ref[...].astype(jnp.float32)
            low = pltpu.roll(field, step, 0)
            high = pltpu.roll(field, points - step, 0)
            for entry in range(entries):
                unit = entry % UNITS
                hits = [jnp.concatenate([mix_ref[section, 3 * entry + j]] * repeat, axis=1) for j in range(3)]
                mixed = (hits[0] * low + hits[1] * field + hits[2] * high).astype(jnp.bfloat16)
                re, im = mixed[:, :coeffs], mixed[:, coeffs:]
                for part in range(2):
                    at = pl.ds((2 * entry + part) * coeffs, coeffs)
                    pltpu.matmul_push_rhs(w_ref[section, at, :], part, unit)
                pltpu.matmul_acc_lhs(sums[2 * unit], re, 0)
                pltpu.matmul_acc_lhs(sums[2 * unit + 1], im)
                pltpu.matmul_acc_lhs(sums[2 * unit], -im, 1)
                pltpu.matmul_acc_lhs(sums[2 * unit + 1], re)
            re = pltpu.matmul_pop(sums[0]) + pltpu.matmul_pop(sums[2])
            im = pltpu.matmul_pop(sums[1]) + pltpu.matmul_pop(sums[3])
            cs, ds = cs_ref[section], ds_ref[section]
            field = jnp.concatenate([re * cs - im * ds, re * ds + im * cs], axis=1).astype(jnp.bfloat16)
            y_ref[...] = field
            for pair in range(pairs):
                out_ref[pair, section, chunk * group : (chunk + 1) * group] = field[pair * group : (pair + 1) * group]
            return carry

        lax.fori_loop(0, sections, one, 0)


def stage(turn, chunk, entries, coeffs, field, weights, mixing, cs, ds, kept):
    flops = 16 * entries * field.shape[0] * coeffs * coeffs

    def body(x_ref, w_ref, mix_ref, cs_ref, ds_ref, kept_ref, y_ref, out_ref):
        sums = [pltpu.ACC(unit)((field.shape[0], coeffs), jnp.float32) for unit in range(UNITS) for _ in range(2)]
        run = functools.partial(
            stage_kernel, turn, chunk, entries, coeffs, x_ref, w_ref, mix_ref, cs_ref, ds_ref, y_ref, out_ref
        )
        pl.run_scoped(run, *sums)

    return pl.pallas_call(
        body,
        out_shape=(jax.ShapeDtypeStruct(field.shape, field.dtype), jax.ShapeDtypeStruct(kept.shape, kept.dtype)),
        in_specs=[VMEM] * 6,
        out_specs=(VMEM, VMEM),
        input_output_aliases={5: 1},
        cost_estimate=pl.CostEstimate(flops=flops, bytes_accessed=weights.size * 2, transcendentals=0),
        compiler_params=LIMIT,
        name="stage",
    )(field, weights, mixing, cs, ds, kept)


def local(initial, props, screen, links, kinds, counts):
    fronts, own_windows, sources, width = initial.shape
    coeffs = width // 2
    entries = props.shape[1]
    columns = lax.axis_size("win")
    sections = lax.axis_size("sec")
    chips = sections // 2
    windows = own_windows * columns
    members = 2 * columns
    points = windows * ROWS
    used = fronts * sources // ROWS
    bf16, f32 = jnp.bfloat16, jnp.float32
    groups = [
        [w * sections + 2 * c + k for w in range(columns) for k in range(2)] for c in range(chips)
    ]

    own = props.reshape(entries * 2 * coeffs, coeffs)
    other = lax.ppermute(own, "sec", [(s, s ^ 1) for s in range(sections)])

    payload, weights = pl.pallas_call(
        functools.partial(pack_kernel, entries),
        out_shape=(
            jax.ShapeDtypeStruct((members, 2 * ROWS, width), bf16),
            jax.ShapeDtypeStruct((2,) + own.shape, bf16),
        ),
        in_specs=[HBM] * 6,
        out_specs=(VMEM, VMEM),
        scratch_shapes=[
            pltpu.VMEM(initial.shape, initial.dtype),
            pltpu.VMEM(screen.shape, screen.dtype),
            pltpu.SMEM(links.shape, links.dtype),
            pltpu.SMEM(kinds.shape, kinds.dtype),
            pltpu.SMEM(counts.shape, counts.dtype),
            pltpu.SemaphoreType.DMA((6,)),
        ],
        compiler_params=LIMIT,
        name="pack",
    )(*[pltpu.with_memory_space_constraint(a, pltpu.HBM) for a in (initial, screen, links, kinds, counts, own)])
    received = lax.all_to_all(payload, ("win", "sec"), 0, 0, axis_index_groups=groups, tiled=True)
    part = points // CHUNKS

    def unpack(received_ref, other_ref, weights_in_ref, *refs):
        unpack_kernel(entries, coeffs, received_ref, other_ref, refs[:CHUNKS], *refs[CHUNKS:])

    *chunks, mixing, cs, ds, weights = pl.pallas_call(
        unpack,
        out_shape=(jax.ShapeDtypeStruct((part, width), bf16),) * CHUNKS
        + (
            jax.ShapeDtypeStruct((2, 3 * entries, part, LANES), f32),
            jax.ShapeDtypeStruct((2, part, coeffs), f32),
            jax.ShapeDtypeStruct((2, part, coeffs), f32),
            jax.ShapeDtypeStruct(weights.shape, bf16),
        ),
        in_specs=[VMEM] * 3,
        out_specs=(VMEM,) * (4 + CHUNKS),
        scratch_shapes=[pltpu.SemaphoreType.DMA],
        input_output_aliases={2: 3 + CHUNKS},
        compiler_params=LIMIT,
        name="unpack",
    )(received, other, weights)

    kept = jnp.zeros((columns, 2, own_windows * ROWS, width), bf16)
    for turn in range(chips):
        for c in range(CHUNKS):
            chunks[c], kept = stage(turn, c, entries, coeffs, chunks[c], weights, mixing, cs, ds, kept)
            if turn + 1 < chips:
                chunks[c] = lax.ppermute(chunks[c], "sec", [(2 * turn + k, 2 * turn + 2 + k) for k in range(2)])

    kept = kept.reshape(members, own_windows * ROWS, width)
    got = lax.all_to_all(kept, ("win", "sec"), 0, 0, axis_index_groups=groups, tiled=True)
    return pl.pallas_call(
        repack_kernel,
        out_shape=jax.ShapeDtypeStruct(initial.shape, bf16),
        in_specs=[VMEM],
        out_specs=VMEM,
        compiler_params=LIMIT,
        name="repack",
    )(got)[None]


def solution(mesh):
    placed = (
        P(None, "win", None, None),
        P("sec", None, None, None, None),
        P("sec", "win", None),
        P("sec", "win", None),
        P("sec", "win", None),
        P("sec", "win"),
    )
    return jax.shard_map(
        local,
        mesh=mesh,
        in_specs=placed,
        out_specs=P("sec", None, "win", None, None),
        check_vma=False,
    )
```

```python
import functools

import jax
import jax.numpy as jnp
from jax import lax
from jax.experimental import pallas as pl
from jax.experimental.pallas import tpu as pltpu
from jax.sharding import PartitionSpec as P

ROWS = 8
LANES = 128
CHUNKS = 2
UNITS = 2
FIRST_PAIR = 8
VMEM = pl.BlockSpec(memory_space=pltpu.VMEM)
HBM = pl.BlockSpec(memory_space=pltpu.HBM)
LIMIT = pltpu.CompilerParams(vmem_limit_bytes=16 << 20)


def pack_kernel(
    entries,
    initial_hbm, screen_hbm, links_hbm, kinds_hbm, counts_hbm, own_hbm, out_ref, weights_ref,
    initial_ref, screen_ref, links_ref, kinds_ref, counts_ref, sems,
):
    copies = [
        pltpu.make_async_copy(source, target, sems.at[i])
        for i, (source, target) in enumerate(
            (
                (counts_hbm, counts_ref),
                (kinds_hbm, kinds_ref),
                (links_hbm, links_ref),
                (screen_hbm, screen_ref),
                (initial_hbm, initial_ref),
                (own_hbm, weights_ref.at[lax.axis_index("sec") % 2]),
            )
        )
    ]
    for copy in copies:
        copy.start()
    for copy in copies[:-1]:
        copy.wait()
    fronts, own_windows, sources, width = initial_ref.shape
    core = lax.axis_index("sec") % 2
    first = lax.axis_index("win") * own_windows
    members = out_ref.shape[0]
    list_length = links_ref.shape[-1]
    per_front = sources // ROWS
    lane = lax.broadcasted_iota(jnp.int32, (1, width), 1)
    trig_rows, hit_rows = [], []
    for w in range(own_windows):
        count = counts_ref[0, w]
        scale = lax.rsqrt(jnp.full((1, width // 2), count, jnp.int32).astype(jnp.float32))
        angle = screen_ref[0, w : w + 1, :]
        trig = jnp.concatenate([jnp.cos(angle) * scale, jnp.sin(angle) * scale], axis=1)
        high = trig.astype(jnp.bfloat16)
        trig_rows += [high, (trig - high.astype(jnp.float32)).astype(jnp.bfloat16)]
        hits = jnp.zeros((1, width), jnp.float32)
        for l in range(list_length):
            spot = kinds_ref[0, w, l] * 3 + links_ref[0, w, l] - (first + w) + 1
            hits = hits + jnp.where((lane == spot) & (l < count), 1.0, 0.0)
        hit_rows.append(hits.astype(jnp.bfloat16))
    spare = jnp.zeros((ROWS - 3 * own_windows, width), jnp.bfloat16)
    tables = jnp.concatenate(trig_rows + hit_rows + [spare], axis=0)
    for member in range(members):
        if member < fronts * per_front:
            f, j = divmod(member, per_front)
            out_ref[member, :ROWS] = initial_ref[f, core, j * ROWS : (j + 1) * ROWS]
        else:
            out_ref[member, :ROWS] = jnp.zeros((ROWS, width), jnp.bfloat16)
        out_ref[member, ROWS:] = tables
    copies[-1].wait()


def unpack_kernel(entries, coeffs, received_ref, tables_at, placed, field_refs, mix_ref, cs_ref, ds_ref, weights_ref, sems):
    copies = [
        pltpu.make_async_copy(source, weights_ref.at[slot], sems.at[i]) for i, (source, slot) in enumerate(placed)
    ]
    for copy in copies:
        copy.start()
    part = ROWS // CHUNKS
    columns = received_ref.shape[0] // 2
    own_windows = 2
    for z in range(columns):
        blocks = [received_ref[2 * z + core].astype(jnp.float32) for core in range(2)]
        at = pl.ds(own_windows * part * z, own_windows * part)
        for chunk, field_ref in enumerate(field_refs):
            rows = [block[chunk * part : (chunk + 1) * part] for block in blocks]
            field_ref[at, :] = jnp.concatenate(rows, axis=0).astype(jnp.bfloat16)
        for core in range(2):
            trigs, hits = [], []
            for w in range(own_windows):
                row = tables_at + 2 * w
                trig = blocks[core][row : row + 1] + blocks[core][row + 1 : row + 2]
                trigs.append(jnp.broadcast_to(trig, (part, 2 * coeffs)))
                row = tables_at + 2 * own_windows + w
                hits.append(jnp.broadcast_to(blocks[core][row : row + 1, :LANES], (part, LANES)))
            trig = jnp.concatenate(trigs, axis=0)
            cs_ref[core, at, :] = trig[:, :coeffs]
            ds_ref[core, at, :] = trig[:, coeffs:]
            hit = jnp.concatenate(hits, axis=0)
            for spot in range(3 * entries):
                mix_ref[core, spot, at, :] = jnp.broadcast_to(hit[:, spot : spot + 1], (own_windows * part, LANES))
    for copy in copies:
        copy.wait()


def repack_kernel(got_ref, out_ref):
    fronts, own_windows, sources, width = out_ref.shape
    per_front = sources // ROWS
    chunks = got_ref.shape[1] // (own_windows * ROWS // CHUNKS)
    part = ROWS // chunks
    for f in range(fronts):
        for j in range(per_front):
            block = got_ref[f * per_front + j].astype(jnp.float32)
            for w in range(own_windows):
                rows = [block[(c * own_windows + w) * part : (c * own_windows + w + 1) * part] for c in range(chunks)]
                out_ref[f, w, j * ROWS : (j + 1) * ROWS] = jnp.concatenate(rows, axis=0).astype(jnp.bfloat16)


def stage_kernel(turn, chunk, entries, coeffs, x_ref, w_ref, mix_ref, cs_ref, ds_ref, y_ref, out_ref, *sums):
    points, width = x_ref.shape
    pairs, sections, group, _ = out_ref.shape
    step = ROWS // CHUNKS
    group = group // CHUNKS
    repeat = width // LANES

    @pl.when(lax.axis_index("sec") // 2 == turn)
    def _():
        y_ref[...] = x_ref[...]

        def one(section, carry):
            field = y_ref[...].astype(jnp.float32)
            low = pltpu.roll(field, step, 0)
            high = pltpu.roll(field, points - step, 0)
            for entry in range(entries):
                unit = entry % UNITS
                hits = [jnp.concatenate([mix_ref[section, 3 * entry + j]] * repeat, axis=1) for j in range(3)]
                mixed = (hits[0] * low + hits[1] * field + hits[2] * high).astype(jnp.bfloat16)
                re, im = mixed[:, :coeffs], mixed[:, coeffs:]
                for part in range(2):
                    at = pl.ds((2 * entry + part) * coeffs, coeffs)
                    pltpu.matmul_push_rhs(w_ref[section, at, :], part, unit)
                pltpu.matmul_acc_lhs(sums[2 * unit], re, 0)
                pltpu.matmul_acc_lhs(sums[2 * unit + 1], im)
                pltpu.matmul_acc_lhs(sums[2 * unit], -im, 1)
                pltpu.matmul_acc_lhs(sums[2 * unit + 1], re)
            re = pltpu.matmul_pop(sums[0]) + pltpu.matmul_pop(sums[2])
            im = pltpu.matmul_pop(sums[1]) + pltpu.matmul_pop(sums[3])
            cs, ds = cs_ref[section], ds_ref[section]
            field = jnp.concatenate([re * cs - im * ds, re * ds + im * cs], axis=1).astype(jnp.bfloat16)
            y_ref[...] = field
            for pair in range(pairs):
                out_ref[pair, section, chunk * group : (chunk + 1) * group] = field[pair * group : (pair + 1) * group]
            return carry

        lax.fori_loop(0, sections, one, 0)


def stage(turn, chunk, entries, coeffs, last, field, weights, mixing, cs, ds, kept):
    flops = 16 * entries * field.shape[0] * coeffs * coeffs

    def body(x_ref, w_ref, mix_ref, cs_ref, ds_ref, kept_ref, *outs):
        out_ref, y_ref = outs if last else outs[::-1]
        sums = [pltpu.ACC(unit)((field.shape[0], coeffs), jnp.float32) for unit in range(UNITS) for _ in range(2)]
        run = functools.partial(
            stage_kernel, turn, chunk, entries, coeffs, x_ref, w_ref, mix_ref, cs_ref, ds_ref, y_ref, out_ref
        )
        pl.run_scoped(run, *sums)

    sent = jax.ShapeDtypeStruct(field.shape, field.dtype)
    results = pl.pallas_call(
        body,
        out_shape=((() if last else (sent,)) + (jax.ShapeDtypeStruct(kept.shape, kept.dtype),)),
        in_specs=[VMEM] * 6,
        out_specs=(VMEM,) * (1 if last else 2),
        scratch_shapes=[pltpu.VMEM(field.shape, field.dtype)] if last else [],
        input_output_aliases={5: 0 if last else 1},
        cost_estimate=pl.CostEstimate(flops=flops, bytes_accessed=weights.size * 2, transcendentals=0),
        compiler_params=LIMIT,
        name="stage",
    )(field, weights, mixing, cs, ds, kept)
    return (None, results[0]) if last else results


def local(initial, props, screen, links, kinds, counts):
    fronts, own_windows, sources, width = initial.shape
    coeffs = width // 2
    entries = props.shape[1]
    columns = lax.axis_size("win")
    sections = lax.axis_size("sec")
    chips = sections // 2
    windows = own_windows * columns
    members = 2 * columns
    points = windows * ROWS
    used = fronts * sources // ROWS
    bf16, f32 = jnp.bfloat16, jnp.float32
    groups = [
        [w * sections + 2 * c + k for w in range(columns) for k in range(2)] for c in range(chips)
    ]

    own = props.reshape(entries * 2 * coeffs, coeffs)
    other = lax.ppermute(own, "sec", [(s, s ^ 1) for s in range(sections)])
    lend = [(c if c % 4 == 2 else c + 1, c + 1 if c % 4 == 2 else c) for c in range(FIRST_PAIR, chips - 2, 2)]
    takers, givers = [t for t, _ in lend], [g for _, g in lend]
    to_taker = [(2 * g + k, 2 * t + k) for t, g in lend for k in range(2)]
    lent = lax.ppermute(own, "sec", to_taker)

    payload, weights = pl.pallas_call(
        functools.partial(pack_kernel, entries),
        out_shape=(
            jax.ShapeDtypeStruct((members, 2 * ROWS, width), bf16),
            jax.ShapeDtypeStruct((2,) + own.shape, bf16),
        ),
        in_specs=[HBM] * 6,
        out_specs=(VMEM, VMEM),
        scratch_shapes=[
            pltpu.VMEM(initial.shape, initial.dtype),
            pltpu.VMEM(screen.shape, screen.dtype),
            pltpu.SMEM(links.shape, links.dtype),
            pltpu.SMEM(kinds.shape, kinds.dtype),
            pltpu.SMEM(counts.shape, counts.dtype),
            pltpu.SemaphoreType.DMA((6,)),
        ],
        compiler_params=LIMIT,
        name="pack",
    )(*[pltpu.with_memory_space_constraint(a, pltpu.HBM) for a in (initial, screen, links, kinds, counts, own)])
    received = lax.all_to_all(payload, ("win", "sec"), 0, 0, axis_index_groups=groups, tiled=True)
    part = points // CHUNKS
    tables = (
        jax.ShapeDtypeStruct((2, 3 * entries, part, LANES), f32),
        jax.ShapeDtypeStruct((2, part, coeffs), f32),
        jax.ShapeDtypeStruct((2, part, coeffs), f32),
        jax.ShapeDtypeStruct(weights.shape, bf16),
    )

    def unpack(received_ref, other_ref, weights_in_ref, *refs):
        placed = [(other_ref, 1 - lax.axis_index("sec") % 2)]
        for member in range(members):
            refs[-2][member] = received_ref[member, ROWS:]
        unpack_kernel(entries, coeffs, received_ref, ROWS, placed, refs[:CHUNKS], *refs[CHUNKS:-2], refs[-1])

    *chunks, mixing, cs, ds, weights, lent_tables = pl.pallas_call(
        unpack,
        out_shape=(jax.ShapeDtypeStruct((part, width), bf16),) * CHUNKS
        + tables
        + (jax.ShapeDtypeStruct((members, ROWS, width), bf16),),
        in_specs=[VMEM] * 3,
        out_specs=(VMEM,) * (5 + CHUNKS),
        scratch_shapes=[pltpu.SemaphoreType.DMA((1,))],
        input_output_aliases={2: 3 + CHUNKS},
        compiler_params=LIMIT,
        name="unpack",
    )(received, other, weights)

    lent_tables = lax.ppermute(lent_tables, "sec", to_taker)

    def among(chip, chosen):
        return functools.reduce(jnp.logical_or, [chip == c for c in chosen])

    def unpack_lent(received_ref, near_ref, far_ref, *refs):
        core = lax.axis_index("sec") % 2

        @pl.when(among(lax.axis_index("sec") // 2, takers))
        def _():
            unpack_kernel(entries, coeffs, received_ref, 0, [(near_ref, core), (far_ref, 1 - core)], (), *refs)

    plan = [(c, "own") for c in range(FIRST_PAIR)]
    for t, g in lend:
        plan += [(t, "own"), (t, "lent")] if t < g else [(t, "lent"), (t, "own")]
    plan += [(c, "own") for c in range(chips - 2, chips)]
    stops = [[plan[0][0], []]]
    for c, kind in plan:
        if stops[-1][0] != c:
            stops.append([c, []])
        stops[-1][1].append(kind)

    kept = {kind: jnp.zeros((columns, 2, own_windows * ROWS, width), bf16) for kind in ("own", "lent")}
    lent_tables, near, weights = lax.optimization_barrier((lent_tables, lent, weights))
    sets = {"own": (weights, mixing, cs, ds)}
    for i, (turn, kinds_here) in enumerate(stops):
        if i == FIRST_PAIR:
            far = lax.ppermute(near, "sec", [(2 * t + k, 2 * t + 1 - k) for t in takers for k in range(2)])
            mixing, cs, ds, weights = pl.pallas_call(
                unpack_lent,
                out_shape=tables,
                in_specs=[VMEM] + [pl.BlockSpec(memory_space=pl.ANY)] * 2,
                out_specs=(VMEM,) * 4,
                scratch_shapes=[pltpu.SemaphoreType.DMA((2,))],
                compiler_params=LIMIT,
                name="unpack_lent",
            )(lent_tables, near, far)
            sets["lent"] = (weights, mixing, cs, ds)
        for c in range(CHUNKS):
            if len(kinds_here) > 1:
                kept["own"], kept["lent"] = lax.optimization_barrier((kept["own"], kept["lent"]))
            for kind in kinds_here:
                last = i + 1 == len(stops) and kind == kinds_here[-1]
                chunks[c], kept[kind] = stage(turn, c, entries, coeffs, last, chunks[c], *sets[kind], kept[kind])
            if i + 1 < len(stops):
                chunks[c] = lax.ppermute(chunks[c], "sec", [(2 * turn + k, 2 * stops[i + 1][0] + k) for k in range(2)])
    kept["own"], kept["lent"] = lax.optimization_barrier((kept["own"], kept["lent"]))
    back = lax.ppermute(kept["lent"], "sec", [(t, g) for g, t in to_taker])
    kept = jnp.where(among(lax.axis_index("sec") // 2, givers), back, kept["own"])

    kept = kept.reshape(members, own_windows * ROWS, width)
    got = lax.all_to_all(kept, ("win", "sec"), 0, 0, axis_index_groups=groups, tiled=True)
    return pl.pallas_call(
        repack_kernel,
        out_shape=jax.ShapeDtypeStruct(initial.shape, bf16),
        in_specs=[VMEM],
        out_specs=VMEM,
        compiler_params=LIMIT,
        name="repack",
    )(got)[None]


def solution(mesh):
    placed = (
        P(None, "win", None, None),
        P("sec", None, None, None, None),
        P("sec", "win", None),
        P("sec", "win", None),
        P("sec", "win", None),
        P("sec", "win"),
    )
    return jax.shard_map(
        local,
        mesh=mesh,
        in_specs=placed,
        out_specs=P("sec", None, "win", None, None),
        check_vma=False,
    )
```

```python
import functools

import jax
import jax.numpy as jnp
from jax import lax
from jax.experimental import pallas as pl
from jax.experimental.pallas import tpu as pltpu
from jax.sharding import PartitionSpec as P

ROWS = 8
LANES = 128
CHUNKS = 2
UNITS = 2
FIRST_PAIR = 8
VMEM = pl.BlockSpec(memory_space=pltpu.VMEM)
HBM = pl.BlockSpec(memory_space=pltpu.HBM)
LIMIT = pltpu.CompilerParams(vmem_limit_bytes=16 << 20)


def pack_kernel(
    entries,
    initial_hbm, screen_hbm, links_hbm, kinds_hbm, counts_hbm, own_hbm, out_ref, weights_ref,
    initial_ref, screen_ref, links_ref, kinds_ref, counts_ref, sems,
):
    copies = [
        pltpu.make_async_copy(source, target, sems.at[i])
        for i, (source, target) in enumerate(
            (
                (counts_hbm, counts_ref),
                (kinds_hbm, kinds_ref),
                (links_hbm, links_ref),
                (screen_hbm, screen_ref),
                (initial_hbm, initial_ref),
                (own_hbm, weights_ref.at[lax.axis_index("sec") % 2]),
            )
        )
    ]
    for copy in copies:
        copy.start()
    for copy in copies[:-1]:
        copy.wait()
    fronts, own_windows, sources, width = initial_ref.shape
    core = lax.axis_index("sec") % 2
    first = lax.axis_index("win") * own_windows
    members = out_ref.shape[0]
    list_length = links_ref.shape[-1]
    per_front = sources // ROWS
    lane = lax.broadcasted_iota(jnp.int32, (1, width), 1)
    trig_rows, hit_rows = [], []
    for w in range(own_windows):
        count = counts_ref[0, w]
        scale = lax.rsqrt(jnp.full((1, width // 2), count, jnp.int32).astype(jnp.float32))
        angle = screen_ref[0, w : w + 1, :]
        trig = jnp.concatenate([jnp.cos(angle) * scale, jnp.sin(angle) * scale], axis=1)
        high = trig.astype(jnp.bfloat16)
        trig_rows += [high, (trig - high.astype(jnp.float32)).astype(jnp.bfloat16)]
        hits = jnp.zeros((1, width), jnp.float32)
        for l in range(list_length):
            spot = kinds_ref[0, w, l] * 3 + links_ref[0, w, l] - (first + w) + 1
            hits = hits + jnp.where((lane == spot) & (l < count), 1.0, 0.0)
        hit_rows.append(hits.astype(jnp.bfloat16))
    spare = jnp.zeros((ROWS - 3 * own_windows, width), jnp.bfloat16)
    tables = jnp.concatenate(trig_rows + hit_rows + [spare], axis=0)
    for member in range(members):
        if member < fronts * per_front:
            f, j = divmod(member, per_front)
            out_ref[member, :ROWS] = initial_ref[f, core, j * ROWS : (j + 1) * ROWS]
        else:
            out_ref[member, :ROWS] = jnp.zeros((ROWS, width), jnp.bfloat16)
        out_ref[member, ROWS:] = tables
    copies[-1].wait()


def unpack_kernel(entries, coeffs, received_ref, tables_at, placed, field_refs, mix_ref, cs_ref, ds_ref, weights_ref, sems):
    copies = [
        pltpu.make_async_copy(source, weights_ref.at[slot], sems.at[i]) for i, (source, slot) in enumerate(placed)
    ]
    for copy in copies:
        copy.start()
    part = ROWS // CHUNKS
    columns = received_ref.shape[0] // 2
    own_windows = 2
    for z in range(columns):
        blocks = [received_ref[2 * z + core].astype(jnp.float32) for core in range(2)]
        at = pl.ds(own_windows * part * z, own_windows * part)
        for chunk, field_ref in enumerate(field_refs):
            rows = [block[chunk * part : (chunk + 1) * part] for block in blocks]
            field_ref[at, :] = jnp.concatenate(rows, axis=0).astype(jnp.bfloat16)
        for core in range(2):
            trigs, hits = [], []
            for w in range(own_windows):
                row = tables_at + 2 * w
                trig = blocks[core][row : row + 1] + blocks[core][row + 1 : row + 2]
                trigs.append(jnp.broadcast_to(trig, (part, 2 * coeffs)))
                row = tables_at + 2 * own_windows + w
                hits.append(jnp.broadcast_to(blocks[core][row : row + 1, :LANES], (part, LANES)))
            trig = jnp.concatenate(trigs, axis=0)
            cs_ref[core, at, :] = trig[:, :coeffs]
            ds_ref[core, at, :] = trig[:, coeffs:]
            hit = jnp.concatenate(hits, axis=0)
            for spot in range(3 * entries):
                mix_ref[core, spot, at, :] = jnp.broadcast_to(hit[:, spot : spot + 1], (own_windows * part, LANES))
    for copy in copies:
        copy.wait()


def repack_kernel(got_ref, out_ref):
    fronts, own_windows, sources, width = out_ref.shape
    per_front = sources // ROWS
    chunks = got_ref.shape[1] // (own_windows * ROWS // CHUNKS)
    part = ROWS // chunks
    for f in range(fronts):
        for j in range(per_front):
            block = got_ref[f * per_front + j].astype(jnp.float32)
            for w in range(own_windows):
                rows = [block[(c * own_windows + w) * part : (c * own_windows + w + 1) * part] for c in range(chunks)]
                out_ref[f, w, j * ROWS : (j + 1) * ROWS] = jnp.concatenate(rows, axis=0).astype(jnp.bfloat16)


def stage_kernel(turn, chunk, entries, coeffs, x_ref, w_ref, mix_ref, cs_ref, ds_ref, y_ref, out_ref, *sums):
    points, width = x_ref.shape
    pairs, sections, group, _ = out_ref.shape
    step = ROWS // CHUNKS
    group = group // CHUNKS
    repeat = width // LANES

    @pl.when(lax.axis_index("sec") // 2 == turn)
    def _():
        y_ref[...] = x_ref[...]

        def one(section, carry):
            field = y_ref[...].astype(jnp.float32)
            low = pltpu.roll(field, step, 0)
            high = pltpu.roll(field, points - step, 0)
            for entry in range(entries):
                unit = entry % UNITS
                hits = [jnp.concatenate([mix_ref[section, 3 * entry + j]] * repeat, axis=1) for j in range(3)]
                mixed = (hits[0] * low + hits[1] * field + hits[2] * high).astype(jnp.bfloat16)
                re, im = mixed[:, :coeffs], mixed[:, coeffs:]
                for part in range(2):
                    at = pl.ds((2 * entry + part) * coeffs, coeffs)
                    pltpu.matmul_push_rhs(w_ref[section, at, :], part, unit)
                pltpu.matmul_acc_lhs(sums[2 * unit], re, 0)
                pltpu.matmul_acc_lhs(sums[2 * unit + 1], im)
                pltpu.matmul_acc_lhs(sums[2 * unit], -im, 1)
                pltpu.matmul_acc_lhs(sums[2 * unit + 1], re)
            re = pltpu.matmul_pop(sums[0]) + pltpu.matmul_pop(sums[2])
            im = pltpu.matmul_pop(sums[1]) + pltpu.matmul_pop(sums[3])
            cs, ds = cs_ref[section], ds_ref[section]
            field = jnp.concatenate([re * cs - im * ds, re * ds + im * cs], axis=1).astype(jnp.bfloat16)
            y_ref[...] = field
            for pair in range(pairs):
                out_ref[pair, section, chunk * group : (chunk + 1) * group] = field[pair * group : (pair + 1) * group]
            return carry

        lax.fori_loop(0, sections, one, 0)


def stage(turn, chunk, entries, coeffs, last, field, weights, mixing, cs, ds, kept):
    flops = 16 * entries * field.shape[0] * coeffs * coeffs

    def body(x_ref, w_ref, mix_ref, cs_ref, ds_ref, kept_ref, *outs):
        out_ref, y_ref = outs if last else outs[::-1]
        sums = [pltpu.ACC(unit)((field.shape[0], coeffs), jnp.float32) for unit in range(UNITS) for _ in range(2)]
        run = functools.partial(
            stage_kernel, turn, chunk, entries, coeffs, x_ref, w_ref, mix_ref, cs_ref, ds_ref, y_ref, out_ref
        )
        pl.run_scoped(run, *sums)

    sent = jax.ShapeDtypeStruct(field.shape, field.dtype)
    results = pl.pallas_call(
        body,
        out_shape=((() if last else (sent,)) + (jax.ShapeDtypeStruct(kept.shape, kept.dtype),)),
        in_specs=[VMEM] * 6,
        out_specs=(VMEM,) * (1 if last else 2),
        scratch_shapes=[pltpu.VMEM(field.shape, field.dtype)] if last else [],
        input_output_aliases={5: 0 if last else 1},
        cost_estimate=pl.CostEstimate(flops=flops, bytes_accessed=weights.size * 2, transcendentals=0),
        compiler_params=LIMIT,
        name="stage",
    )(field, weights, mixing, cs, ds, kept)
    return (None, results[0]) if last else results


def local(initial, props, screen, links, kinds, counts):
    fronts, own_windows, sources, width = initial.shape
    coeffs = width // 2
    entries = props.shape[1]
    columns = lax.axis_size("win")
    sections = lax.axis_size("sec")
    chips = sections // 2
    windows = own_windows * columns
    members = 2 * columns
    points = windows * ROWS
    used = fronts * sources // ROWS
    bf16, f32 = jnp.bfloat16, jnp.float32
    groups = [
        [w * sections + 2 * c + k for w in range(columns) for k in range(2)] for c in range(chips)
    ]

    own = props.reshape(entries * 2 * coeffs, coeffs)
    other = lax.ppermute(own, "sec", [(s, s ^ 1) for s in range(sections)])
    lend = [(c if c % 4 == 2 else c + 1, c + 1 if c % 4 == 2 else c) for c in range(FIRST_PAIR, chips - 2, 2)]
    takers, givers = [t for t, _ in lend], [g for _, g in lend]
    to_taker = [(2 * g + k, 2 * t + k) for t, g in lend for k in range(2)]
    lent = lax.ppermute(own, "sec", to_taker)

    payload, weights = pl.pallas_call(
        functools.partial(pack_kernel, entries),
        out_shape=(
            jax.ShapeDtypeStruct((members, 2 * ROWS, width), bf16),
            jax.ShapeDtypeStruct((2,) + own.shape, bf16),
        ),
        in_specs=[HBM] * 6,
        out_specs=(VMEM, VMEM),
        scratch_shapes=[
            pltpu.VMEM(initial.shape, initial.dtype),
            pltpu.VMEM(screen.shape, screen.dtype),
            pltpu.SMEM(links.shape, links.dtype),
            pltpu.SMEM(kinds.shape, kinds.dtype),
            pltpu.SMEM(counts.shape, counts.dtype),
            pltpu.SemaphoreType.DMA((6,)),
        ],
        compiler_params=LIMIT,
        name="pack",
    )(*[pltpu.with_memory_space_constraint(a, pltpu.HBM) for a in (initial, screen, links, kinds, counts, own)])
    received = lax.all_to_all(payload, ("win", "sec"), 0, 0, axis_index_groups=groups, tiled=True)
    part = points // CHUNKS
    tables = (
        jax.ShapeDtypeStruct((2, 3 * entries, part, LANES), f32),
        jax.ShapeDtypeStruct((2, part, coeffs), f32),
        jax.ShapeDtypeStruct((2, part, coeffs), f32),
        jax.ShapeDtypeStruct(weights.shape, bf16),
    )

    def unpack(received_ref, other_ref, weights_in_ref, *refs):
        placed = [(other_ref, 1 - lax.axis_index("sec") % 2)]
        for member in range(members):
            refs[-2][member] = received_ref[member, ROWS:]
        unpack_kernel(entries, coeffs, received_ref, ROWS, placed, refs[:CHUNKS], *refs[CHUNKS:-2], refs[-1])

    *chunks, mixing, cs, ds, weights, lent_tables = pl.pallas_call(
        unpack,
        out_shape=(jax.ShapeDtypeStruct((part, width), bf16),) * CHUNKS
        + tables
        + (jax.ShapeDtypeStruct((members, ROWS, width), bf16),),
        in_specs=[VMEM] * 3,
        out_specs=(VMEM,) * (5 + CHUNKS),
        scratch_shapes=[pltpu.SemaphoreType.DMA((1,))],
        input_output_aliases={2: 3 + CHUNKS},
        compiler_params=LIMIT,
        name="unpack",
    )(received, other, weights)

    lent_tables = lax.ppermute(lent_tables, "sec", to_taker)

    def among(chip, chosen):
        return functools.reduce(jnp.logical_or, [chip == c for c in chosen])

    def unpack_lent(received_ref, near_ref, far_ref, *refs):
        core = lax.axis_index("sec") % 2

        @pl.when(among(lax.axis_index("sec") // 2, takers))
        def _():
            unpack_kernel(entries, coeffs, received_ref, 0, [(near_ref, core), (far_ref, 1 - core)], (), *refs)

    plan = [(c, "own") for c in range(FIRST_PAIR)]
    for t, g in lend:
        plan += [(t, "own"), (t, "lent")] if t < g else [(t, "lent"), (t, "own")]
    plan += [(c, "own") for c in range(chips - 2, chips)]
    stops = [[plan[0][0], []]]
    for c, kind in plan:
        if stops[-1][0] != c:
            stops.append([c, []])
        stops[-1][1].append(kind)

    kept = {kind: jnp.zeros((columns, 2, own_windows * ROWS, width), bf16) for kind in ("own", "lent")}
    near, weights = lax.optimization_barrier((lent, weights))
    sets = {"own": (weights, mixing, cs, ds)}
    for i, (turn, kinds_here) in enumerate(stops):
        if i == FIRST_PAIR:
            far = lax.ppermute(near, "sec", [(2 * t + k, 2 * t + 1 - k) for t in takers for k in range(2)])
            mixing, cs, ds, weights = pl.pallas_call(
                unpack_lent,
                out_shape=tables,
                in_specs=[VMEM] + [pl.BlockSpec(memory_space=pl.ANY)] * 2,
                out_specs=(VMEM,) * 4,
                scratch_shapes=[pltpu.SemaphoreType.DMA((2,))],
                compiler_params=LIMIT,
                name="unpack_lent",
            )(lent_tables, near, far)
            sets["lent"] = (weights, mixing, cs, ds)
        for c in range(CHUNKS):
            if len(kinds_here) > 1:
                kept["own"], kept["lent"] = lax.optimization_barrier((kept["own"], kept["lent"]))
            for kind in kinds_here:
                last = i + 1 == len(stops) and kind == kinds_here[-1]
                chunks[c], kept[kind] = stage(turn, c, entries, coeffs, last, chunks[c], *sets[kind], kept[kind])
            if i + 1 < len(stops):
                chunks[c] = lax.ppermute(chunks[c], "sec", [(2 * turn + k, 2 * stops[i + 1][0] + k) for k in range(2)])
    kept["own"], kept["lent"] = lax.optimization_barrier((kept["own"], kept["lent"]))
    back = lax.ppermute(kept["lent"], "sec", [(t, g) for g, t in to_taker])
    kept = jnp.where(among(lax.axis_index("sec") // 2, givers), back, kept["own"])

    kept = kept.reshape(members, own_windows * ROWS, width)
    got = lax.all_to_all(kept, ("win", "sec"), 0, 0, axis_index_groups=groups, tiled=True)
    return pl.pallas_call(
        repack_kernel,
        out_shape=jax.ShapeDtypeStruct(initial.shape, bf16),
        in_specs=[VMEM],
        out_specs=VMEM,
        compiler_params=LIMIT,
        name="repack",
    )(got)[None]


def solution(mesh):
    placed = (
        P(None, "win", None, None),
        P("sec", None, None, None, None),
        P("sec", "win", None),
        P("sec", "win", None),
        P("sec", "win", None),
        P("sec", "win"),
    )
    return jax.shard_map(
        local,
        mesh=mesh,
        in_specs=placed,
        out_specs=P("sec", None, "win", None, None),
        check_vma=False,
    )
```

```python
import functools

import jax
import jax.numpy as jnp
from jax import lax
from jax.experimental import pallas as pl
from jax.experimental.pallas import tpu as pltpu
from jax.sharding import PartitionSpec as P

ROWS = 8
LANES = 128
CHUNKS = 2
UNITS = 2
FIRST_PAIR = 8
VMEM = pl.BlockSpec(memory_space=pltpu.VMEM)
HBM = pl.BlockSpec(memory_space=pltpu.HBM)
LIMIT = pltpu.CompilerParams(vmem_limit_bytes=16 << 20)


def pack_kernel(
    entries,
    initial_hbm, screen_hbm, links_hbm, kinds_hbm, counts_hbm, out_ref,
    initial_ref, screen_ref, links_ref, kinds_ref, counts_ref, sems,
):
    copies = [
        pltpu.make_async_copy(source, target, sems.at[i])
        for i, (source, target) in enumerate(
            (
                (counts_hbm, counts_ref),
                (kinds_hbm, kinds_ref),
                (links_hbm, links_ref),
                (screen_hbm, screen_ref),
                (initial_hbm, initial_ref),
            )
        )
    ]
    for copy in copies:
        copy.start()
    for copy in copies:
        copy.wait()
    fronts, own_windows, sources, width = initial_ref.shape
    core = lax.axis_index("sec") % 2
    first = lax.axis_index("win") * own_windows
    members = out_ref.shape[0]
    list_length = links_ref.shape[-1]
    per_front = sources // ROWS
    lane = lax.broadcasted_iota(jnp.int32, (1, width), 1)
    trig_rows, hit_rows = [], []
    for w in range(own_windows):
        count = counts_ref[0, w]
        scale = lax.rsqrt(jnp.full((1, width // 2), count, jnp.int32).astype(jnp.float32))
        angle = screen_ref[0, w : w + 1, :]
        trig = jnp.concatenate([jnp.cos(angle) * scale, jnp.sin(angle) * scale], axis=1)
        high = trig.astype(jnp.bfloat16)
        trig_rows += [high, (trig - high.astype(jnp.float32)).astype(jnp.bfloat16)]
        hits = jnp.zeros((1, width), jnp.float32)
        for l in range(list_length):
            spot = kinds_ref[0, w, l] * 3 + links_ref[0, w, l] - (first + w) + 1
            hits = hits + jnp.where((lane == spot) & (l < count), 1.0, 0.0)
        hit_rows.append(hits.astype(jnp.bfloat16))
    spare = jnp.zeros((ROWS - 3 * own_windows, width), jnp.bfloat16)
    tables = jnp.concatenate(trig_rows + hit_rows + [spare], axis=0)
    for member in range(members):
        if member < fronts * per_front:
            f, j = divmod(member, per_front)
            out_ref[member, :ROWS] = initial_ref[f, core, j * ROWS : (j + 1) * ROWS]
        else:
            out_ref[member, :ROWS] = jnp.zeros((ROWS, width), jnp.bfloat16)
        out_ref[member, ROWS:] = tables


def unpack_kernel(entries, coeffs, received_ref, tables_at, placed, field_refs, mix_ref, cs_ref, ds_ref, weights_ref, sems):
    copies = [
        pltpu.make_async_copy(source, weights_ref.at[slot], sems.at[i]) for i, (source, slot) in enumerate(placed)
    ]
    for copy in copies:
        copy.start()
    part = ROWS // CHUNKS
    columns = received_ref.shape[0] // 2
    own_windows = 2
    for z in range(columns):
        blocks = [received_ref[2 * z + core].astype(jnp.float32) for core in range(2)]
        at = pl.ds(own_windows * part * z, own_windows * part)
        for chunk, field_ref in enumerate(field_refs):
            rows = [block[chunk * part : (chunk + 1) * part] for block in blocks]
            field_ref[at, :] = jnp.concatenate(rows, axis=0).astype(jnp.bfloat16)
        for core in range(2):
            trigs, hits = [], []
            for w in range(own_windows):
                row = tables_at + 2 * w
                trig = blocks[core][row : row + 1] + blocks[core][row + 1 : row + 2]
                trigs.append(jnp.broadcast_to(trig, (part, 2 * coeffs)))
                row = tables_at + 2 * own_windows + w
                hits.append(jnp.broadcast_to(blocks[core][row : row + 1, :LANES], (part, LANES)))
            trig = jnp.concatenate(trigs, axis=0)
            cs_ref[core, at, :] = trig[:, :coeffs]
            ds_ref[core, at, :] = trig[:, coeffs:]
            hit = jnp.concatenate(hits, axis=0)
            for spot in range(3 * entries):
                mix_ref[core, spot, at, :] = jnp.broadcast_to(hit[:, spot : spot + 1], (own_windows * part, LANES))
    for copy in copies:
        copy.wait()


def repack_kernel(got_ref, out_ref):
    fronts, own_windows, sources, width = out_ref.shape
    per_front = sources // ROWS
    chunks = got_ref.shape[1] // (own_windows * ROWS // CHUNKS)
    part = ROWS // chunks
    for f in range(fronts):
        for j in range(per_front):
            block = got_ref[f * per_front + j].astype(jnp.float32)
            for w in range(own_windows):
                rows = [block[(c * own_windows + w) * part : (c * own_windows + w + 1) * part] for c in range(chunks)]
                out_ref[f, w, j * ROWS : (j + 1) * ROWS] = jnp.concatenate(rows, axis=0).astype(jnp.bfloat16)


def stage_kernel(turn, chunk, entries, coeffs, x_ref, w_ref, mix_ref, cs_ref, ds_ref, y_ref, out_ref, *sums):
    points, width = x_ref.shape
    pairs, sections, group, _ = out_ref.shape
    step = ROWS // CHUNKS
    group = group // CHUNKS
    repeat = width // LANES

    @pl.when(lax.axis_index("sec") // 2 == turn)
    def _():
        y_ref[...] = x_ref[...]

        def one(section, carry):
            field = y_ref[...].astype(jnp.float32)
            low = pltpu.roll(field, step, 0)
            high = pltpu.roll(field, points - step, 0)
            for entry in range(entries):
                unit = entry % UNITS
                hits = [jnp.concatenate([mix_ref[section, 3 * entry + j]] * repeat, axis=1) for j in range(3)]
                mixed = (hits[0] * low + hits[1] * field + hits[2] * high).astype(jnp.bfloat16)
                re, im = mixed[:, :coeffs], mixed[:, coeffs:]
                for part in range(2):
                    at = pl.ds((2 * entry + part) * coeffs, coeffs)
                    pltpu.matmul_push_rhs(w_ref[section, at, :], part, unit)
                pltpu.matmul_acc_lhs(sums[2 * unit], re, 0)
                pltpu.matmul_acc_lhs(sums[2 * unit + 1], im)
                pltpu.matmul_acc_lhs(sums[2 * unit], -im, 1)
                pltpu.matmul_acc_lhs(sums[2 * unit + 1], re)
            re = pltpu.matmul_pop(sums[0]) + pltpu.matmul_pop(sums[2])
            im = pltpu.matmul_pop(sums[1]) + pltpu.matmul_pop(sums[3])
            cs, ds = cs_ref[section], ds_ref[section]
            field = jnp.concatenate([re * cs - im * ds, re * ds + im * cs], axis=1).astype(jnp.bfloat16)
            y_ref[...] = field
            for pair in range(pairs):
                out_ref[pair, section, chunk * group : (chunk + 1) * group] = field[pair * group : (pair + 1) * group]
            return carry

        lax.fori_loop(0, sections, one, 0)


def stage(turn, chunk, entries, coeffs, last, field, weights, mixing, cs, ds, kept):
    flops = 16 * entries * field.shape[0] * coeffs * coeffs

    def body(x_ref, w_ref, mix_ref, cs_ref, ds_ref, kept_ref, *outs):
        out_ref, y_ref = outs if last else outs[::-1]
        sums = [pltpu.ACC(unit)((field.shape[0], coeffs), jnp.float32) for unit in range(UNITS) for _ in range(2)]
        run = functools.partial(
            stage_kernel, turn, chunk, entries, coeffs, x_ref, w_ref, mix_ref, cs_ref, ds_ref, y_ref, out_ref
        )
        pl.run_scoped(run, *sums)

    sent = jax.ShapeDtypeStruct(field.shape, field.dtype)
    results = pl.pallas_call(
        body,
        out_shape=((() if last else (sent,)) + (jax.ShapeDtypeStruct(kept.shape, kept.dtype),)),
        in_specs=[VMEM] * 6,
        out_specs=(VMEM,) * (1 if last else 2),
        scratch_shapes=[pltpu.VMEM(field.shape, field.dtype)] if last else [],
        input_output_aliases={5: 0 if last else 1},
        cost_estimate=pl.CostEstimate(flops=flops, bytes_accessed=weights.size * 2, transcendentals=0),
        compiler_params=LIMIT,
        name="stage",
    )(field, weights, mixing, cs, ds, kept)
    return (None, results[0]) if last else results


def local(initial, props, screen, links, kinds, counts):
    fronts, own_windows, sources, width = initial.shape
    coeffs = width // 2
    entries = props.shape[1]
    columns = lax.axis_size("win")
    sections = lax.axis_size("sec")
    chips = sections // 2
    windows = own_windows * columns
    members = 2 * columns
    points = windows * ROWS
    used = fronts * sources // ROWS
    bf16, f32 = jnp.bfloat16, jnp.float32
    groups = [
        [w * sections + 2 * c + k for w in range(columns) for k in range(2)] for c in range(chips)
    ]

    own = props.reshape(entries * 2 * coeffs, coeffs)
    other = lax.ppermute(own, "sec", [(s, s ^ 1) for s in range(sections)])
    lend = [(c if c % 4 == 2 else c + 1, c + 1 if c % 4 == 2 else c) for c in range(FIRST_PAIR, chips - 2, 2)]
    takers, givers = [t for t, _ in lend], [g for _, g in lend]
    to_taker = [(2 * g + k, 2 * t + k) for t, g in lend for k in range(2)]
    lent = lax.ppermute(own, "sec", to_taker)

    payload = pl.pallas_call(
        functools.partial(pack_kernel, entries),
        out_shape=jax.ShapeDtypeStruct((members, 2 * ROWS, width), bf16),
        in_specs=[HBM] * 5,
        out_specs=VMEM,
        scratch_shapes=[
            pltpu.VMEM(initial.shape, initial.dtype),
            pltpu.VMEM(screen.shape, screen.dtype),
            pltpu.SMEM(links.shape, links.dtype),
            pltpu.SMEM(kinds.shape, kinds.dtype),
            pltpu.SMEM(counts.shape, counts.dtype),
            pltpu.SemaphoreType.DMA((5,)),
        ],
        compiler_params=LIMIT,
        name="pack",
    )(*[pltpu.with_memory_space_constraint(a, pltpu.HBM) for a in (initial, screen, links, kinds, counts)])
    received = lax.all_to_all(payload, ("win", "sec"), 0, 0, axis_index_groups=groups, tiled=True)
    part = points // CHUNKS
    tables = (
        jax.ShapeDtypeStruct((2, 3 * entries, part, LANES), f32),
        jax.ShapeDtypeStruct((2, part, coeffs), f32),
        jax.ShapeDtypeStruct((2, part, coeffs), f32),
        jax.ShapeDtypeStruct((2,) + own.shape, bf16),
    )

    def unpack(received_ref, other_ref, own_ref, *refs):
        core = lax.axis_index("sec") % 2
        placed = [(own_ref, core), (other_ref, 1 - core)]
        for member in range(members):
            refs[-2][member] = received_ref[member, ROWS:]
        unpack_kernel(entries, coeffs, received_ref, ROWS, placed, refs[:CHUNKS], *refs[CHUNKS:-2], refs[-1])

    *chunks, mixing, cs, ds, weights, lent_tables = pl.pallas_call(
        unpack,
        out_shape=(jax.ShapeDtypeStruct((part, width), bf16),) * CHUNKS
        + tables
        + (jax.ShapeDtypeStruct((members, ROWS, width), bf16),),
        in_specs=[VMEM, VMEM, HBM],
        out_specs=(VMEM,) * (5 + CHUNKS),
        scratch_shapes=[pltpu.SemaphoreType.DMA((2,))],
        compiler_params=LIMIT,
        name="unpack",
    )(received, other, pltpu.with_memory_space_constraint(own, pltpu.HBM))

    lent_tables = lax.ppermute(lent_tables, "sec", to_taker)

    def among(chip, chosen):
        return functools.reduce(jnp.logical_or, [chip == c for c in chosen])

    def unpack_lent(received_ref, near_ref, far_ref, *refs):
        core = lax.axis_index("sec") % 2

        @pl.when(among(lax.axis_index("sec") // 2, takers))
        def _():
            unpack_kernel(entries, coeffs, received_ref, 0, [(near_ref, core), (far_ref, 1 - core)], (), *refs)

    plan = [(c, "own") for c in range(FIRST_PAIR)]
    for t, g in lend:
        plan += [(t, "own"), (t, "lent")] if t < g else [(t, "lent"), (t, "own")]
    plan += [(c, "own") for c in range(chips - 2, chips)]
    stops = [[plan[0][0], []]]
    for c, kind in plan:
        if stops[-1][0] != c:
            stops.append([c, []])
        stops[-1][1].append(kind)

    kept = {kind: jnp.zeros((columns, 2, own_windows * ROWS, width), bf16) for kind in ("own", "lent")}
    near, weights = lax.optimization_barrier((lent, weights))
    sets = {"own": (weights, mixing, cs, ds)}
    for i, (turn, kinds_here) in enumerate(stops):
        if i == FIRST_PAIR:
            far = lax.ppermute(near, "sec", [(2 * t + k, 2 * t + 1 - k) for t in takers for k in range(2)])
            mixing, cs, ds, weights = pl.pallas_call(
                unpack_lent,
                out_shape=tables,
                in_specs=[VMEM] + [pl.BlockSpec(memory_space=pl.ANY)] * 2,
                out_specs=(VMEM,) * 4,
                scratch_shapes=[pltpu.SemaphoreType.DMA((2,))],
                compiler_params=LIMIT,
                name="unpack_lent",
            )(lent_tables, near, far)
            sets["lent"] = (weights, mixing, cs, ds)
        for c in range(CHUNKS):
            if len(kinds_here) > 1:
                kept["own"], kept["lent"] = lax.optimization_barrier((kept["own"], kept["lent"]))
            for kind in kinds_here:
                last = i + 1 == len(stops) and kind == kinds_here[-1]
                chunks[c], kept[kind] = stage(turn, c, entries, coeffs, last, chunks[c], *sets[kind], kept[kind])
            if i + 1 < len(stops):
                chunks[c] = lax.ppermute(chunks[c], "sec", [(2 * turn + k, 2 * stops[i + 1][0] + k) for k in range(2)])
    kept["own"], kept["lent"] = lax.optimization_barrier((kept["own"], kept["lent"]))
    back = lax.ppermute(kept["lent"], "sec", [(t, g) for g, t in to_taker])
    kept = jnp.where(among(lax.axis_index("sec") // 2, givers), back, kept["own"])

    kept = kept.reshape(members, own_windows * ROWS, width)
    got = lax.all_to_all(kept, ("win", "sec"), 0, 0, axis_index_groups=groups, tiled=True)
    return pl.pallas_call(
        repack_kernel,
        out_shape=jax.ShapeDtypeStruct(initial.shape, bf16),
        in_specs=[VMEM],
        out_specs=VMEM,
        compiler_params=LIMIT,
        name="repack",
    )(got)[None]


def solution(mesh):
    placed = (
        P(None, "win", None, None),
        P("sec", None, None, None, None),
        P("sec", "win", None),
        P("sec", "win", None),
        P("sec", "win", None),
        P("sec", "win"),
    )
    return jax.shard_map(
        local,
        mesh=mesh,
        in_specs=placed,
        out_specs=P("sec", None, "win", None, None),
        check_vma=False,
    )
```
